32 devices in a mesh: seq: 8 (over z, core), res: 4 (over y, x).
Axes of the slice: x: 2, y: 2, z: 4, core: 2. Of those that a mesh axis runs over, the one named last changes fastest.
Arguments:
- alignment_embedding: bfloat16 [64, 1024, 256], P('seq', 'res'), may hold values from -6 to 6
- unscaled_edge_prior: bfloat16 [8, 1024, 1024], P(None, 'res', 'seq'), may hold values from -6 to 6
- edge_prior_factor: float32 [8], replicated, may hold values from 0.5 to 3
- horizontal_standardize_factor: float32 [256], replicated, may hold values from 0.25 to 1.75
- horizontal_probe_lookup: bfloat16 [2, 256, 256], replicated, may hold values from -15 to 15
- horizontal_content_switch: bfloat16 [2, 256, 256], replicated, may hold values from -0.375 to 0.375
- horizontal_sigmoid_shift: float32 [256], replicated, may hold values from -4 to 4
- horizontal_final_matrix: bfloat16 [256, 256], replicated, may hold values from -0.375 to 0.375
- vertical_standardize_factor: float32 [256], replicated, may hold values from 0.25 to 1.75
- vertical_probe_lookup: bfloat16 [2, 256, 256], replicated, may hold values from -15 to 15
- vertical_content_switch: bfloat16 [2, 256, 256], replicated, may hold values from -0.375 to 0.375
- vertical_sigmoid_shift: float32 [256], replicated, may hold values from -4 to 4
- vertical_final_matrix: bfloat16 [256, 256], replicated, may hold values from -0.375 to 0.375
Outputs:
- msa_out: float32 [64, 1024, 256], P('seq', 'res')
The draws below stay inside these ranges and needn't reach their ends.
All inputs are finite; a program needn't handle non-finite values.
Results may differ from the reference program's by a relative error of at most 0.04.
The reference program's roundings to bfloat16 on the way count: a program that leaves them out, or rounds other values in their place, can miss the bound.
Values may be sent and summed in bfloat16 or wider, within the bound.
No kernel may reach another device: no remote copies, remote signals or barrier semaphores. Data moves between devices by JAX's collectives and lax.ppermute only.
A program may use at most 128 MiB of HBM per device.

```python
import math
import jax
import jax.numpy as jnp
from jax import lax

FEATURE_DEPTH = 256
LEARNER_NUMBER = 8
SUBSPACE_WIDTH = 32
ALIGNED_AMOUNT = 64
POSITION_AMOUNT = 1024


def qk_pair(key, deviation):
    starting_point = jax.random.normal(key, (2, FEATURE_DEPTH, LEARNER_NUMBER * SUBSPACE_WIDTH), jnp.float32) * (deviation / math.sqrt(FEATURE_DEPTH))
    starting_point = jnp.clip(starting_point, -6.0 * deviation / math.sqrt(FEATURE_DEPTH), 6.0 * deviation / math.sqrt(FEATURE_DEPTH))
    return starting_point.astype(jnp.bfloat16)


def draw_horizontal_probe_lookup(key, part):
    return qk_pair(jax.random.fold_in(key, 11), 1.5)


def draw_vertical_probe_lookup(key, part):
    return qk_pair(jax.random.fold_in(key, 13), 2.5)


def levels(stream_key, dims, pieces, low, top_value):
    gain, own = 1.0, jax.random.fold_in(stream_key, 6)
    for dim, blocks in pieces:
        steps = jnp.exp(jax.random.uniform(jax.random.fold_in(own, dim), (blocks,), jnp.float32, low / len(pieces), top_value / len(pieces)))
        gain = gain * jnp.repeat(steps, dims[dim] // blocks).reshape([-1 if axis == dim else 1 for axis in range(len(dims))])
    return gain


def gaussian(key, dims, scale, limit, split=(), kind=jnp.bfloat16):
    gain = levels(key, dims, split, -0.22, 0.18) if split else 1.0
    drawn = jax.random.normal(key, dims, jnp.float32) * scale * gain
    return jnp.minimum(jnp.maximum(drawn, -limit), limit).astype(kind)


def setup_inputs(seed: int = 0) -> dict:
    arg_keys = jax.random.split(jax.random.key(seed), 14)
    alignment_embedding = gaussian(arg_keys[0], (ALIGNED_AMOUNT, POSITION_AMOUNT, FEATURE_DEPTH), 1.0, 6.0, ((0, 8), (1, 4)))
    unscaled_edge_prior = gaussian(arg_keys[1], (LEARNER_NUMBER, POSITION_AMOUNT, POSITION_AMOUNT), 1.0, 6.0, ((1, 4), (2, 8)))
    edge_prior_factor = jnp.clip(jnp.exp(jax.random.uniform(arg_keys[2], (LEARNER_NUMBER,), jnp.float32, math.log(0.5), math.log(3.0))), 0.5, 3.0)
    horizontal_standardize_factor = jnp.clip(1.0 + 0.15 * jax.random.normal(arg_keys[3], (FEATURE_DEPTH,), jnp.float32), 0.25, 1.75)
    horizontal_probe_lookup = draw_horizontal_probe_lookup(jax.random.fold_in(arg_keys[13], 71), 0)
    horizontal_content_switch = gaussian(arg_keys[5], (2, FEATURE_DEPTH, LEARNER_NUMBER * SUBSPACE_WIDTH), FEATURE_DEPTH ** -0.5, 0.375)
    horizontal_sigmoid_shift = gaussian(arg_keys[6], (LEARNER_NUMBER * SUBSPACE_WIDTH,), 1.0, 4.0, (), jnp.float32)
    horizontal_final_matrix = gaussian(arg_keys[7], (LEARNER_NUMBER * SUBSPACE_WIDTH, FEATURE_DEPTH), (LEARNER_NUMBER * SUBSPACE_WIDTH) ** -0.5, 0.375)
    vertical_standardize_factor = jnp.clip(1.0 + 0.15 * jax.random.normal(arg_keys[8], (FEATURE_DEPTH,), jnp.float32), 0.25, 1.75)
    vertical_probe_lookup = draw_vertical_probe_lookup(jax.random.fold_in(arg_keys[13], 71), 0)
    vertical_content_switch = gaussian(arg_keys[10], (2, FEATURE_DEPTH, LEARNER_NUMBER * SUBSPACE_WIDTH), FEATURE_DEPTH ** -0.5, 0.375)
    vertical_sigmoid_shift = gaussian(arg_keys[11], (LEARNER_NUMBER * SUBSPACE_WIDTH,), 1.0, 4.0, (), jnp.float32)
    vertical_final_matrix = gaussian(arg_keys[12], (LEARNER_NUMBER * SUBSPACE_WIDTH, FEATURE_DEPTH), (LEARNER_NUMBER * SUBSPACE_WIDTH) ** -0.5, 0.375)
    return dict(alignment_embedding=alignment_embedding, unscaled_edge_prior=unscaled_edge_prior, edge_prior_factor=edge_prior_factor, horizontal_standardize_factor=horizontal_standardize_factor, horizontal_probe_lookup=horizontal_probe_lookup, horizontal_content_switch=horizontal_content_switch, horizontal_sigmoid_shift=horizontal_sigmoid_shift, horizontal_final_matrix=horizontal_final_matrix, vertical_standardize_factor=vertical_standardize_factor, vertical_probe_lookup=vertical_probe_lookup, vertical_content_switch=vertical_content_switch, vertical_sigmoid_shift=vertical_sigmoid_shift, vertical_final_matrix=vertical_final_matrix)


EPS = 1e-05

def lower_precision(array):
    return lax.optimization_barrier(array.astype(jnp.bfloat16))

def standardize_features(row_data, standardize_factor):
    row_data = row_data.astype(jnp.float32)
    row_mean = lax.optimization_barrier(jnp.mean(row_data, -1, keepdims=True))
    centred = row_data - row_mean
    deviation = lax.optimization_barrier(jnp.mean(centred * centred, -1, keepdims=True))
    return lower_precision(centred * lax.rsqrt(deviation + EPS) * standardize_factor)

def linear_transform(array, weight):
    return jnp.einsum('...c,cf->...f', array.astype(jnp.float32), weight.astype(jnp.float32))

def horizontal_focus_path(alignment_embedding, unscaled_edge_prior, edge_prior_factor, standardize_factor, probe_lookup_matrix, content_switch_matrix, sigmoid_shift_array, final_matrix):
    position_number = alignment_embedding.shape[1]
    head_count = edge_prior_factor.shape[0]
    proj_width = probe_lookup_matrix.shape[2]
    head_size = proj_width // head_count
    scaled_bias = unscaled_edge_prior.astype(jnp.float32) * edge_prior_factor[:, None, None]
    standardized_source = standardize_features(alignment_embedding, standardize_factor)

    def one_sequence(seq_rows):
        queries = lower_precision(linear_transform(seq_rows, probe_lookup_matrix[0])).reshape(position_number, head_count, head_size)
        key_part = lower_precision(linear_transform(seq_rows, probe_lookup_matrix[1])).reshape(position_number, head_count, head_size)
        values = lower_precision(linear_transform(seq_rows, content_switch_matrix[0])).reshape(position_number, head_count, head_size)
        gates = jax.nn.sigmoid(linear_transform(seq_rows, content_switch_matrix[1]) + sigmoid_shift_array)
        scores = jnp.einsum('ihd,jhd->hij', queries.astype(jnp.float32), key_part.astype(jnp.float32)) / math.sqrt(head_size) + scaled_bias
        row_max = lax.optimization_barrier(jnp.max(scores, -1, keepdims=True))
        weights = jnp.exp(scores - row_max)
        totals = lax.optimization_barrier(jnp.sum(weights, -1))
        focused_result = jnp.einsum('hij,jhd->ihd', lower_precision(weights).astype(jnp.float32), values.astype(jnp.float32)) / totals.T[:, :, None]
        return lower_precision(focused_result.reshape(position_number, proj_width) * gates)
    focused_result = lax.map(one_sequence, standardized_source)
    return alignment_embedding.astype(jnp.float32) + linear_transform(focused_result, final_matrix)

def column_branch(combined_subspaces, standardize_factor, probe_lookup_matrix, content_switch_matrix, sigmoid_shift_array, final_matrix, head_count):
    seq_total, position_number, feature_number = combined_subspaces.shape
    proj_width = probe_lookup_matrix.shape[2]
    head_size = proj_width // head_count
    blocks = combined_subspaces.transpose(1, 0, 2).reshape(position_number // 16, 16, seq_total, feature_number)

    def one_block(block_rows):
        standardized_source = standardize_features(block_rows, standardize_factor)
        queries = lower_precision(linear_transform(standardized_source, probe_lookup_matrix[0])).reshape(16, seq_total, head_count, head_size)
        key_part = lower_precision(linear_transform(standardized_source, probe_lookup_matrix[1])).reshape(16, seq_total, head_count, head_size)
        values = lower_precision(linear_transform(standardized_source, content_switch_matrix[0])).reshape(16, seq_total, head_count, head_size)
        gates = jax.nn.sigmoid(linear_transform(standardized_source, content_switch_matrix[1]) + sigmoid_shift_array)
        scores = jnp.einsum('rshd,rthd->rhst', queries.astype(jnp.float32), key_part.astype(jnp.float32)) / math.sqrt(head_size)
        row_max = lax.optimization_barrier(jnp.max(scores, -1, keepdims=True))
        weights = jnp.exp(scores - row_max)
        totals = lax.optimization_barrier(jnp.sum(weights, -1))
        focused_result = jnp.einsum('rhst,rthd->rshd', lower_precision(weights).astype(jnp.float32), values.astype(jnp.float32)) / totals.transpose(0, 2, 1)[:, :, :, None]
        focused_result = lower_precision(focused_result.reshape(16, seq_total, proj_width) * gates)
        return block_rows.astype(jnp.float32) + linear_transform(focused_result, final_matrix)
    result = lax.map(one_block, blocks)
    return result.reshape(position_number, seq_total, feature_number).transpose(1, 0, 2)

def reference(alignment_embedding, unscaled_edge_prior, edge_prior_factor, horizontal_standardize_factor, horizontal_probe_lookup, horizontal_content_switch, horizontal_sigmoid_shift, horizontal_final_matrix, vertical_standardize_factor, vertical_probe_lookup, vertical_content_switch, vertical_sigmoid_shift, vertical_final_matrix):
    combined_subspaces = horizontal_focus_path(alignment_embedding, unscaled_edge_prior, edge_prior_factor, horizontal_standardize_factor, horizontal_probe_lookup, horizontal_content_switch, horizontal_sigmoid_shift, horizontal_final_matrix)
    return column_branch(combined_subspaces, vertical_standardize_factor, vertical_probe_lookup, vertical_content_switch, vertical_sigmoid_shift, vertical_final_matrix, edge_prior_factor.shape[0])
```

```python
import functools
import math

import jax
import jax.numpy as jnp
from jax import lax
from jax.experimental import pallas as pl
from jax.experimental.pallas import tpu as pltpu
from jax.sharding import PartitionSpec as P

EPS = 1e-05
LOG2E = math.log2(math.e)
BF, F32 = jnp.bfloat16, jnp.float32
NN = (((1,), (0,)), ((), ()))
NT = (((1,), (1,)), ((), ()))
TN = (((0,), (0,)), ((), ()))
LANES = 128
ONES = 16
KEY_CHUNK = 512
ROW_CHUNKS = 2
COL_CHUNKS = 2


def dot(a, b, dims=NN):
    return lax.dot_general(a, b, dims, preferred_element_type=F32)


def params(limit=None):
    return pltpu.CompilerParams(dimension_semantics=("arbitrary",), vmem_limit_bytes=limit)


def cost(flops, nbytes):
    return pl.CostEstimate(flops=int(flops), bytes_accessed=int(nbytes), transcendentals=0)


def standardize(rows, gain):
    centred = rows - jnp.mean(rows, -1, keepdims=True)
    deviation = jnp.mean(centred * centred, -1, keepdims=True)
    return centred * lax.rsqrt(deviation + EPS) * gain


def whole(array):
    return pl.BlockSpec(
        array.shape, lambda *_: (0,) * array.ndim, pipeline_mode=pl.Buffered(1)
    )


def head_mask(tile, place, size):
    owner = lax.broadcasted_iota(jnp.int32, (tile.shape[0], 1), 0) // size
    return jnp.where(owner == place, tile, jnp.zeros_like(tile))


def project_kernel(size, own, x_ref, gain, wk, wv_t, wq_t, wg_t, shift, k_out, v_out, *rest):
    normed = standardize(x_ref[0].astype(F32), gain[...]).astype(BF)
    k_out[0] = dot(normed, wk[...]).astype(BF)
    values = dot(wv_t[...], normed, NT).astype(BF)
    heads, rows, count = v_out.shape[1:]
    for h in range(heads):
        v_out[0, h, :size] = values[h * size : (h + 1) * size]
        v_out[0, h, size:] = jnp.ones((rows - size, count), BF)
    if own:
        q_out, g_out = rest
        scale = LOG2E / math.sqrt(size)
        q_out[0] = (dot(wq_t[...], normed, NT) * scale).astype(BF)
        g_out[0] = jax.nn.sigmoid(dot(wg_t[...], normed, NT) + shift[...])


def project(x, weights, heads, own):
    members, count, features = x.shape
    width = weights[1].shape[1]
    size = width // heads
    rows = size + ONES
    out = [
        jax.ShapeDtypeStruct((members, count, width), BF),
        jax.ShapeDtypeStruct((members, heads, rows, count), BF),
    ]
    specs = [
        pl.BlockSpec((1, count, width), lambda s: (s, 0, 0)),
        pl.BlockSpec((1, heads, rows, count), lambda s: (s, 0, 0, 0)),
    ]
    if own:
        out += [
            jax.ShapeDtypeStruct((members, width, count), BF),
            jax.ShapeDtypeStruct((members, width, count), F32),
        ]
        specs += [pl.BlockSpec((1, width, count), lambda s: (s, 0, 0))] * 2
    return pl.pallas_call(
        functools.partial(project_kernel, size, own),
        grid=(members,),
        in_specs=[pl.BlockSpec((1, count, features), lambda s: (s, 0, 0))]
        + [whole(w) for w in weights],
        out_specs=specs,
        out_shape=out,
        compiler_params=params(),
        cost_estimate=cost(2 * x.size * width * (4 if own else 2), x.size * 8),
        name="project_own" if own else "project",
    )(x, *weights)


def row_kernel(blocks, parts, size, place, factor, me, *refs):
    x_ref, q_ref, g_ref, wo = refs[:4]
    keys = refs[4 : 4 + blocks]
    values = refs[4 + blocks : 4 + 2 * blocks]
    priors = refs[4 + 2 * blocks : 4 + 2 * blocks + parts]
    outs = refs[4 + 2 * blocks + parts : 4 + 2 * blocks + 2 * parts]
    bias_s, score_s, mixed_s = refs[4 + 2 * blocks + 2 * parts :]
    heads, count, width = bias_s.shape
    block = keys[0].shape[1]
    piece = count // parts

    @pl.when(pl.program_id(0) == 0)
    def _():
        for p in range(parts):
            rows = pl.ds(pl.multiple_of(place[p] * piece, piece), piece)
            for h in range(heads):
                bias_s[h, rows, :] = priors[p][h].astype(F32) * (factor[h] * LOG2E)

    per = LANES // size
    chunk = min(KEY_CHUNK, count)
    each = min(chunk, block)
    attended, top, queries = [], None, None
    for h in range(heads + 1):
        total, high = None, None
        if h < heads:
            group = slice(h // per * LANES, (h // per + 1) * LANES)
            queries = head_mask(q_ref[0, group, :], h % per, size)
        for c in range(count // chunk):
            rows = slice(c * chunk, (c + 1) * chunk)
            places = [divmod(c * chunk + e, block) for e in range(0, chunk, each)]
            if h < heads:
                part = jnp.concatenate([keys[b][0, o : o + each, group] for b, o in places], 0)
                scores = dot(part, queries) + bias_s[h, rows, :]
                score_s[h % 2, rows, :] = scores
                best = jnp.max(scores.reshape(chunk // 8, 8, width), axis=0)
                high = best if high is None else jnp.maximum(high, best)
            if h > 0:
                weights = jnp.exp2(score_s[(h - 1) % 2, rows, :] - top).astype(BF)
                part = jnp.concatenate([values[b][0, h - 1, :, o : o + each] for b, o in places], 1)
                term = dot(part, weights)
                total = term if total is None else total + term
        if h > 0:
            gate = g_ref[0, (h - 1) * size : h * size, :]
            attended.append((total[:size] / total[size : size + 1] * gate).astype(BF))
        if h < heads:
            top = jnp.max(high, axis=0, keepdims=True)
    joined = jnp.concatenate(attended, 0)
    mixed_s[...] = x_ref[0].astype(F32) + dot(joined, wo[...], TN)
    sub = outs[0].shape[1]
    for k in range(parts):
        dest = lax.rem(me[0] + k, parts)
        outs[k][0] = mixed_s[pl.ds(pl.multiple_of(dest * sub, sub), sub), :].astype(BF)


def row_attention(place, factor, me, x, q, g, wo, keys, values, priors, first, members):
    blocks, parts = len(keys), len(priors)
    heads = factor.shape[0]
    _, count, features = x.shape
    width = q.shape[1]
    size = width // heads
    total = blocks * count
    pick3 = lambda s, *_: (first + s, 0, 0)
    pick4 = lambda s, *_: (first + s, 0, 0, 0)
    sub = count // parts
    grid_spec = pltpu.PrefetchScalarGridSpec(
        num_scalar_prefetch=3,
        grid=(members,),
        in_specs=[
            pl.BlockSpec((1, count, features), pick3),
            pl.BlockSpec((1, width, count), pick3),
            pl.BlockSpec((1, width, count), pick3),
            whole(wo),
        ]
        + [pl.BlockSpec((1,) + k.shape[1:], pick3) for k in keys]
        + [pl.BlockSpec((1,) + v.shape[1:], pick4) for v in values]
        + [whole(b) for b in priors],
        out_specs=[pl.BlockSpec((1, sub, features), lambda s, *_: (s, 0, 0))] * parts,
        scratch_shapes=[
            pltpu.VMEM((heads, total, count), F32),
            pltpu.VMEM((2, total, count), F32),
            pltpu.VMEM((count, features), F32),
        ],
    )
    work = 2 * members * total * count * width * 16
    return pl.pallas_call(
        functools.partial(row_kernel, blocks, parts, size),
        grid_spec=grid_spec,
        out_shape=[jax.ShapeDtypeStruct((members, sub, features), BF)] * parts,
        compiler_params=params(60 << 20),
        cost_estimate=cost(work, priors[0].size * parts * 2),
        name="row_attention",
    )(place, factor, me, x, q, g, wo, *keys, *values, *priors)


def column_kernel(slots, heads, *refs):
    xs = refs[:slots]
    gain, wk, wv_t, wq_t, wg_t, shift, wo = refs[slots : slots + 7]
    outs = refs[slots + 7 : 2 * slots + 7]
    x_s, n_s, o_s = refs[2 * slots + 7 :]
    members, residues, features = xs[0].shape
    width = wk.shape[1]
    size = width // heads
    each = members * residues
    rows = slots * each
    seqs = slots * members
    for k in range(slots):
        x_s[k * each : (k + 1) * each, :] = xs[k][...].astype(F32).reshape(each, features)
    normed = standardize(x_s[...], gain[...])
    tiles = range(features // LANES)
    for i in tiles:
        n_s[i] = normed[:, i * LANES : (i + 1) * LANES]

    def strided(ref, r):
        return jnp.concatenate([ref[i, pl.ds(r, seqs, stride=residues), :] for i in tiles], 1)

    normed = jnp.concatenate([strided(n_s, r).astype(BF) for r in range(residues)], 0)
    scale = LOG2E / math.sqrt(size)
    keys = dot(normed, wk[...]).astype(BF)
    values = dot(wv_t[...], normed, NT).astype(BF)
    queries = (dot(wq_t[...], normed, NT) * scale).astype(BF)
    gates = jax.nn.sigmoid(dot(wg_t[...], normed, NT) + shift[...])
    join = max(1, LANES // seqs)
    span = join * seqs
    per = LANES // size
    ones = jnp.ones((ONES, span), BF)
    lane = lax.broadcasted_iota(jnp.int32, (1, span), 1) // seqs
    for t in range(residues // join):
        cols = slice(t * span, (t + 1) * span)
        attended = []
        for h in range(heads):
            group = slice(h // per * LANES, (h // per + 1) * LANES)
            crossed = dot(keys[cols, group], head_mask(queries[group, cols], h % per, size))
            scores = crossed[:seqs]
            for i in range(1, join):
                scores = jnp.where(lane == i, crossed[i * seqs : (i + 1) * seqs], scores)
            weights = jnp.exp2(scores - jnp.max(scores, axis=0, keepdims=True))
            spread = [jnp.where(lane == i, weights, 0.0) for i in range(join)]
            spread = jnp.concatenate(spread, 0).astype(BF)
            part = jnp.concatenate([values[h * size : (h + 1) * size, cols], ones], 0)
            total = dot(part, spread)
            gate = gates[h * size : (h + 1) * size, cols]
            attended.append((total[:size] / total[size : size + 1] * gate).astype(BF))
        update = dot(jnp.concatenate(attended, 0), wo[...], TN)
        for i in range(join):
            pick = pl.ds(t * join + i, seqs, stride=residues)
            for j in tiles:
                part = update[i * seqs : (i + 1) * seqs, j * LANES : (j + 1) * LANES]
                o_s[j, pick, :] = part
    for k in range(slots):
        at = slice(k * each, (k + 1) * each)
        rows = x_s[at, :] + jnp.concatenate([o_s[j, at, :] for j in tiles], 1)
        outs[k][...] = rows.astype(BF).reshape(members, residues, features)


def column_attention(xs, weights, heads, first, residues):
    slots = len(xs)
    members, _, features = xs[0].shape
    step = 8
    rows = slots * members * step
    offset = first // step
    return pl.pallas_call(
        functools.partial(column_kernel, slots, heads),
        grid=(residues // step,),
        in_specs=[pl.BlockSpec((members, step, features), lambda r: (0, offset + r, 0))] * slots
        + [whole(w) for w in weights],
        out_specs=[pl.BlockSpec((members, step, features), lambda r: (0, r, 0))] * slots,
        out_shape=[jax.ShapeDtypeStruct((members, residues, features), BF)] * slots,
        scratch_shapes=[pltpu.VMEM((rows, features), F32)]
        + [pltpu.VMEM((features // LANES, rows, LANES), F32)] * 2,
        compiler_params=params(60 << 20),
        cost_estimate=cost(2 * rows // step * residues * features * features * 30, rows * 8),
        name="column_attention",
    )(*xs, *weights)


def assemble_kernel(parts, chunks, me, *refs):
    blocks, out = refs[:-1], refs[-1]
    rows = blocks[0].shape[1]
    for k in range(parts):
        dest = lax.rem(me[0] + k, parts)
        for c in range(chunks):
            at = pl.multiple_of((dest * chunks + c) * rows, rows)
            out[0, pl.ds(at, rows), :] = blocks[k * chunks + c][0].astype(F32)


def assemble(me, blocks, parts, chunks):
    members, rows, features = blocks[0].shape
    count = rows * chunks * parts
    grid_spec = pltpu.PrefetchScalarGridSpec(
        num_scalar_prefetch=1,
        grid=(members,),
        in_specs=[pl.BlockSpec((1, rows, features), lambda s, *_: (s, 0, 0))] * len(blocks),
        out_specs=pl.BlockSpec((1, count, features), lambda s, *_: (s, 0, 0)),
    )
    return pl.pallas_call(
        functools.partial(assemble_kernel, parts, chunks),
        grid_spec=grid_spec,
        out_shape=jax.ShapeDtypeStruct((members, count, features), F32),
        compiler_params=params(),
        cost_estimate=cost(0, members * count * features * 6),
        name="assemble",
    )(me, *blocks)


def shards(
    alignment_embedding,
    unscaled_edge_prior,
    edge_prior_factor,
    horizontal_standardize_factor,
    horizontal_probe_lookup,
    horizontal_content_switch,
    horizontal_sigmoid_shift,
    horizontal_final_matrix,
    vertical_standardize_factor,
    vertical_probe_lookup,
    vertical_content_switch,
    vertical_sigmoid_shift,
    vertical_final_matrix,
):
    x = alignment_embedding
    members, count, features = x.shape
    heads = edge_prior_factor.shape[0]
    parts, blocks = lax.axis_size("seq"), lax.axis_size("res")
    seq, res = lax.axis_index("seq"), lax.axis_index("res")
    piece = unscaled_edge_prior.shape[2]

    def swap(array, bits):
        return lax.ppermute(array, "res", [(i, i ^ bits) for i in range(blocks)])

    def shift(array, step):
        return lax.ppermute(array, "seq", [(i, (i + step) % parts) for i in range(parts)])

    def partner(array):
        return lax.ppermute(array, "seq", [(i, i ^ 1) for i in range(parts)])

    x_slots = [x] + [swap(x, m) for m in range(1, blocks)]
    prior = jnp.swapaxes(unscaled_edge_prior, 1, 2)
    priors = [prior] + [shift(prior, 2 * k) for k in range(1, parts // 2)]
    priors = priors + [partner(p) for p in priors]
    owners = [(seq - 2 * k) % parts for k in range(parts // 2)]
    owners = jnp.stack(owners + [((seq ^ 1) - 2 * k) % parts for k in range(parts // 2)])
    per = count // piece
    place = ((owners // per) ^ res) * per + owners % per

    def prepared(gain, probe, switch, offset):
        return (
            gain[None],
            probe[1],
            switch[0].T,
            probe[0].T,
            switch[1].T,
            offset[:, None],
        )

    weights = prepared(
        horizontal_standardize_factor,
        horizontal_probe_lookup,
        horizontal_content_switch,
        horizontal_sigmoid_shift,
    )
    keys, values = [None] * blocks, [None] * blocks
    keys[0], values[0], queries, gates = project(x_slots[0], weights, heads, True)
    for m in range(1, blocks):
        keys[m], values[m] = project(x_slots[m], weights, heads, False)
    place, me = place.astype(jnp.int32), seq.astype(jnp.int32)[None]
    columns = [[] for _ in range(parts)]
    chunk = members // ROW_CHUNKS
    for c in range(ROW_CHUNKS):
        pieces = row_attention(
            place,
            edge_prior_factor,
            me,
            x,
            queries,
            gates,
            horizontal_final_matrix,
            keys,
            values,
            priors,
            c * chunk,
            chunk,
        )
        for k in range(parts):
            columns[k].append(pieces[k] if k == 0 else shift(pieces[k], k))
    flat = [block for slot in columns for block in slot]
    weights = prepared(
        vertical_standardize_factor,
        vertical_probe_lookup,
        vertical_content_switch,
        vertical_sigmoid_shift,
    ) + (vertical_final_matrix,)
    sub = count // parts
    span = sub // COL_CHUNKS
    back = [[None] * COL_CHUNKS for _ in range(parts)]
    for c in range(COL_CHUNKS):
        results = column_attention(flat, weights, heads, c * span, span)
        for k in range(parts):
            joined = jnp.concatenate(results[k * ROW_CHUNKS : (k + 1) * ROW_CHUNKS], 0)
            back[k][c] = joined if k == 0 else shift(joined, -k)
    return assemble(me, [b for slot in back for b in slot], parts, COL_CHUNKS)


def solution(mesh):
    placed = (P("seq", "res", None), P(None, "res", "seq")) + (P(),) * 11
    return jax.shard_map(
        shards, mesh=mesh, in_specs=placed, out_specs=P("seq", "res", None), check_vma=False
    )
```

```python
import functools
import math

import jax
import jax.numpy as jnp
from jax import lax
from jax.experimental import pallas as pl
from jax.experimental.pallas import tpu as pltpu
from jax.sharding import PartitionSpec as P

EPS = 1e-05
LOG2E = math.log2(math.e)
BF, F32 = jnp.bfloat16, jnp.float32
NN = (((1,), (0,)), ((), ()))
NT = (((1,), (1,)), ((), ()))
TN = (((0,), (0,)), ((), ()))
LANES = 128
ONES = 16
KEY_CHUNK = 512
ROW_CHUNKS = 2
COL_CHUNKS = 2


def dot(a, b, dims=NN):
    return lax.dot_general(a, b, dims, preferred_element_type=F32)


def params(limit=None):
    return pltpu.CompilerParams(dimension_semantics=("arbitrary",), vmem_limit_bytes=limit)


def cost(flops, nbytes):
    return pl.CostEstimate(flops=int(flops), bytes_accessed=int(nbytes), transcendentals=0)


def standardize(rows, gain):
    centred = rows - jnp.mean(rows, -1, keepdims=True)
    deviation = jnp.mean(centred * centred, -1, keepdims=True)
    return centred * lax.rsqrt(deviation + EPS) * gain


def whole(array):
    return pl.BlockSpec(
        array.shape, lambda *_: (0,) * array.ndim, pipeline_mode=pl.Buffered(1)
    )


def head_mask(tile, place, size):
    owner = lax.broadcasted_iota(jnp.int32, (tile.shape[0], 1), 0) // size
    return jnp.where(owner == place, tile, jnp.zeros_like(tile))


def project_kernel(size, own, x_ref, gain, wk, wv_t, wq_t, wg_t, shift, k_out, v_out, *rest):
    members, count, features = x_ref.shape
    rows = x_ref[...].astype(F32).reshape(members * count, features)
    normed = standardize(rows, gain[...]).astype(BF)
    k_out[...] = dot(normed, wk[...]).astype(BF).reshape(k_out.shape)
    values = dot(wv_t[...], normed, NT).astype(BF)
    heads, depth = v_out.shape[1:3]
    ones = jnp.ones((depth - size, count), BF)
    if own:
        q_out, g_out = rest
        queries = (dot(wq_t[...], normed, NT) * (LOG2E / math.sqrt(size))).astype(BF)
        gates = jax.nn.sigmoid(dot(wg_t[...], normed, NT) + shift[...])
    for s in range(members):
        at = slice(s * count, (s + 1) * count)
        for h in range(heads):
            v_out[s, h, :size] = values[h * size : (h + 1) * size, at]
            v_out[s, h, size:] = ones
        if own:
            q_out[s] = queries[:, at]
            g_out[s] = gates[:, at]


def project(x, weights, heads, own):
    members, count, features = x.shape
    width = weights[1].shape[1]
    size = width // heads
    rows = size + ONES
    step = math.gcd(members, 4)
    pick3 = lambda s: (s, 0, 0)
    out = [
        jax.ShapeDtypeStruct((members, count, width), BF),
        jax.ShapeDtypeStruct((members, heads, rows, count), BF),
    ]
    specs = [
        pl.BlockSpec((step, count, width), pick3),
        pl.BlockSpec((step, heads, rows, count), lambda s: (s, 0, 0, 0)),
    ]
    if own:
        out += [
            jax.ShapeDtypeStruct((members, width, count), BF),
            jax.ShapeDtypeStruct((members, width, count), F32),
        ]
        specs += [pl.BlockSpec((step, width, count), pick3)] * 2
    return pl.pallas_call(
        functools.partial(project_kernel, size, own),
        grid=(members // step,),
        in_specs=[pl.BlockSpec((step, count, features), pick3)] + [whole(w) for w in weights],
        out_specs=specs,
        out_shape=out,
        compiler_params=params(60 << 20),
        cost_estimate=cost(2 * x.size * width * (4 if own else 2), x.size * 8),
        name="project_own" if own else "project",
    )(x, *weights)


def row_kernel(blocks, parts, size, place, factor, *refs):
    x_ref, q_ref, g_ref, wo = refs[:4]
    keys = refs[4 : 4 + blocks]
    values = refs[4 + blocks : 4 + 2 * blocks]
    priors = refs[4 + 2 * blocks : 4 + 2 * blocks + parts]
    out, bias_s, score_s = refs[4 + 2 * blocks + parts :]
    heads, count, width = bias_s.shape
    block = keys[0].shape[1]
    piece = count // parts

    @pl.when(pl.program_id(0) == 0)
    def _():
        for p in range(parts):
            rows = pl.ds(pl.multiple_of(place[p] * piece, piece), piece)
            for h in range(heads):
                bias_s[h, rows, :] = priors[p][h].astype(F32) * (factor[h] * LOG2E)

    per = LANES // size
    chunk = min(KEY_CHUNK, count)
    each = min(chunk, block)
    attended, top, queries = [], None, None
    for h in range(heads + 1):
        total, high = None, None
        if h < heads:
            group = slice(h // per * LANES, (h // per + 1) * LANES)
            queries = head_mask(q_ref[0, group, :], h % per, size)
        for c in range(count // chunk):
            rows = slice(c * chunk, (c + 1) * chunk)
            places = [divmod(c * chunk + e, block) for e in range(0, chunk, each)]
            if h < heads:
                part = jnp.concatenate([keys[b][0, o : o + each, group] for b, o in places], 0)
                scores = dot(part, queries) + bias_s[h, rows, :]
                score_s[h % 2, rows, :] = scores
                best = jnp.max(scores.reshape(chunk // 8, 8, width), axis=0)
                high = best if high is None else jnp.maximum(high, best)
            if h > 0:
                weights = jnp.exp2(score_s[(h - 1) % 2, rows, :] - top).astype(BF)
                part = jnp.concatenate([values[b][0, h - 1, :, o : o + each] for b, o in places], 1)
                term = dot(part, weights)
                total = term if total is None else total + term
        if h > 0:
            gate = g_ref[0, (h - 1) * size : h * size, :]
            attended.append((total[:size] / total[size : size + 1] * gate).astype(BF))
        if h < heads:
            top = jnp.max(high, axis=0, keepdims=True)
    joined = jnp.concatenate(attended, 0)
    mixed = x_ref[0].astype(F32) + dot(joined, wo[...], TN)
    out[:, 0] = mixed.astype(BF).reshape(parts, out.shape[2], mixed.shape[1])


def row_attention(place, factor, x, q, g, wo, keys, values, priors, first, members):
    blocks, parts = len(keys), len(priors)
    heads = factor.shape[0]
    _, count, features = x.shape
    width = q.shape[1]
    size = width // heads
    total = blocks * count
    pick3 = lambda s, *_: (first + s, 0, 0)
    pick4 = lambda s, *_: (first + s, 0, 0, 0)
    sub = count // parts
    grid_spec = pltpu.PrefetchScalarGridSpec(
        num_scalar_prefetch=2,
        grid=(members,),
        in_specs=[
            pl.BlockSpec((1, count, features), pick3),
            pl.BlockSpec((1, width, count), pick3),
            pl.BlockSpec((1, width, count), pick3),
            whole(wo),
        ]
        + [pl.BlockSpec((1,) + k.shape[1:], pick3) for k in keys]
        + [pl.BlockSpec((1,) + v.shape[1:], pick4) for v in values]
        + [whole(b) for b in priors],
        out_specs=pl.BlockSpec((parts, 1, sub, features), lambda s, *_: (0, s, 0, 0)),
        scratch_shapes=[
            pltpu.VMEM((heads, total, count), F32),
            pltpu.VMEM((2, total, count), F32),
        ],
    )
    work = 2 * members * total * count * width * 16
    return pl.pallas_call(
        functools.partial(row_kernel, blocks, parts, size),
        grid_spec=grid_spec,
        out_shape=jax.ShapeDtypeStruct((parts, members, sub, features), BF),
        compiler_params=params(60 << 20),
        cost_estimate=cost(work, priors[0].size * parts * 2),
        name="row_attention",
    )(place, factor, x, q, g, wo, *keys, *values, *priors)


def column_kernel(chunks, heads, *refs):
    xs = refs[:chunks]
    gain, wk, wv_t, wq_t, wg_t, shift, wo = refs[chunks : chunks + 7]
    out, x_s, n_s, o_s = refs[chunks + 7 :]
    parts, members, residues, features = xs[0].shape
    slots = parts * chunks
    width = wk.shape[1]
    size = width // heads
    each = members * residues
    rows = slots * each
    seqs = slots * members
    for k in range(slots):
        block = xs[k % chunks][k // chunks].astype(F32)
        x_s[k * each : (k + 1) * each, :] = block.reshape(each, features)
    normed = standardize(x_s[...], gain[...])
    tiles = range(features // LANES)
    for i in tiles:
        n_s[i] = normed[:, i * LANES : (i + 1) * LANES]

    def strided(ref, r):
        return jnp.concatenate([ref[i, pl.ds(r, seqs, stride=residues), :] for i in tiles], 1)

    normed = jnp.concatenate([strided(n_s, r).astype(BF) for r in range(residues)], 0)
    scale = LOG2E / math.sqrt(size)
    keys = dot(normed, wk[...]).astype(BF)
    values = dot(wv_t[...], normed, NT).astype(BF)
    queries = (dot(wq_t[...], normed, NT) * scale).astype(BF)
    gates = jax.nn.sigmoid(dot(wg_t[...], normed, NT) + shift[...])
    join = max(1, LANES // seqs)
    span = join * seqs
    per = LANES // size
    ones = jnp.ones((ONES, span), BF)
    lane = lax.broadcasted_iota(jnp.int32, (1, span), 1) // seqs
    for t in range(residues // join):
        cols = slice(t * span, (t + 1) * span)
        attended = []
        for h in range(heads):
            group = slice(h // per * LANES, (h // per + 1) * LANES)
            crossed = dot(keys[cols, group], head_mask(queries[group, cols], h % per, size))
            scores = crossed[:seqs]
            for i in range(1, join):
                scores = jnp.where(lane == i, crossed[i * seqs : (i + 1) * seqs], scores)
            weights = jnp.exp2(scores - jnp.max(scores, axis=0, keepdims=True))
            spread = [jnp.where(lane == i, weights, 0.0) for i in range(join)]
            spread = jnp.concatenate(spread, 0).astype(BF)
            part = jnp.concatenate([values[h * size : (h + 1) * size, cols], ones], 0)
            total = dot(part, spread)
            gate = gates[h * size : (h + 1) * size, cols]
            attended.append((total[:size] / total[size : size + 1] * gate).astype(BF))
        update = dot(jnp.concatenate(attended, 0), wo[...], TN)
        for i in range(join):
            pick = pl.ds(t * join + i, seqs, stride=residues)
            for j in tiles:
                part = update[i * seqs : (i + 1) * seqs, j * LANES : (j + 1) * LANES]
                o_s[j, pick, :] = part
    for k in range(slots):
        at = slice(k * each, (k + 1) * each)
        rows = x_s[at, :] + jnp.concatenate([o_s[j, at, :] for j in tiles], 1)
        at = slice(k % chunks * members, (k % chunks + 1) * members)
        out[k // chunks, at] = rows.astype(BF).reshape(members, residues, features)


def column_attention(xs, weights, heads, first, residues):
    chunks = len(xs)
    parts, members, _, features = xs[0].shape
    step = 8
    rows = parts * chunks * members * step
    offset = first // step
    return pl.pallas_call(
        functools.partial(column_kernel, chunks, heads),
        grid=(residues // step,),
        in_specs=[
            pl.BlockSpec((parts, members, step, features), lambda r: (0, 0, offset + r, 0))
        ]
        * chunks
        + [whole(w) for w in weights],
        out_specs=pl.BlockSpec(
            (parts, members * chunks, step, features), lambda r: (0, 0, r, 0)
        ),
        out_shape=jax.ShapeDtypeStruct((parts, members * chunks, residues, features), BF),
        scratch_shapes=[pltpu.VMEM((rows, features), F32)]
        + [pltpu.VMEM((features // LANES, rows, LANES), F32)] * 2,
        compiler_params=params(60 << 20),
        cost_estimate=cost(2 * rows // step * residues * features * features * 30, rows * 8),
        name="column_attention",
    )(*xs, *weights)


def assemble_kernel(*refs):
    blocks, out = refs[:-1], refs[-1]
    parts, _, rows, _ = blocks[0].shape
    for k in range(parts):
        for c, block in enumerate(blocks):
            at = (k * len(blocks) + c) * rows
            out[:, at : at + rows, :] = block[k].astype(F32)


def assemble(blocks):
    parts, members, rows, features = blocks[0].shape
    count = rows * len(blocks) * parts
    step = min(4, members)
    return pl.pallas_call(
        assemble_kernel,
        grid=(members // step,),
        in_specs=[pl.BlockSpec((parts, step, rows, features), lambda s: (0, s, 0, 0))]
        * len(blocks),
        out_specs=pl.BlockSpec((step, count, features), lambda s: (s, 0, 0)),
        out_shape=jax.ShapeDtypeStruct((members, count, features), F32),
        compiler_params=params(),
        cost_estimate=cost(0, members * count * features * 6),
        name="assemble",
    )(*blocks)


def shards(
    alignment_embedding,
    unscaled_edge_prior,
    edge_prior_factor,
    horizontal_standardize_factor,
    horizontal_probe_lookup,
    horizontal_content_switch,
    horizontal_sigmoid_shift,
    horizontal_final_matrix,
    vertical_standardize_factor,
    vertical_probe_lookup,
    vertical_content_switch,
    vertical_sigmoid_shift,
    vertical_final_matrix,
):
    x = alignment_embedding
    members, count, features = x.shape
    heads = edge_prior_factor.shape[0]
    parts, blocks = lax.axis_size("seq"), lax.axis_size("res")
    seq, res = lax.axis_index("seq"), lax.axis_index("res")
    piece = unscaled_edge_prior.shape[2]

    def swap(array, bits):
        return lax.ppermute(array, "res", [(i, i ^ bits) for i in range(blocks)])

    def shift(array, step):
        return lax.ppermute(array, "seq", [(i, (i + step) % parts) for i in range(parts)])

    def partner(array):
        return lax.ppermute(array, "seq", [(i, i ^ 1) for i in range(parts)])

    near = [swap(x, 1 << b) for b in range(blocks.bit_length() - 1)]
    prior = jnp.swapaxes(unscaled_edge_prior, 1, 2)
    priors = [prior] + [shift(prior, 2 * k) for k in range(1, parts // 2)]
    owners = [(seq - 2 * k) % parts for k in range(parts // 2)]
    owners = jnp.stack(owners + [((seq ^ 1) - 2 * k) % parts for k in range(parts // 2)])
    per = count // piece
    place = ((owners // per) ^ res) * per + owners % per

    def prepared(gain, probe, switch, offset):
        return (
            gain[None],
            probe[1],
            switch[0].T,
            probe[0].T,
            switch[1].T,
            offset[:, None],
        )

    weights = prepared(
        horizontal_standardize_factor,
        horizontal_probe_lookup,
        horizontal_content_switch,
        horizontal_sigmoid_shift,
    )
    keys, values = [None] * blocks, [None] * blocks
    keys[0], values[0], queries, gates = project(x, weights, heads, True)
    half = members // 2
    if blocks == 4:
        far = jnp.concatenate([swap(near[0][:half], 2), swap(near[1][half:], 1)], 0)
        x_slots = [x, near[0], near[1], far]
    else:
        bits = {1 << b: rows for b, rows in enumerate(near)}
        x_slots = [x] + [bits[m] if m in bits else swap(x, m) for m in range(1, blocks)]
    for m in range(1, blocks):
        if m == blocks - 1:
            held = tuple(k for k in keys if k is not None)
            priors, held = lax.optimization_barrier((priors, held))
            keys[: len(held)] = held
            priors = priors + [partner(p) for p in priors]
        keys[m], values[m] = project(x_slots[m], weights, heads, False)
    place = place.astype(jnp.int32)
    exchange = functools.partial(
        lax.all_to_all, axis_name="seq", split_axis=0, concat_axis=0, tiled=True
    )
    columns = []
    chunk = members // ROW_CHUNKS
    for c in range(ROW_CHUNKS):
        mixed = row_attention(
            place,
            edge_prior_factor,
            x,
            queries,
            gates,
            horizontal_final_matrix,
            keys,
            values,
            priors,
            c * chunk,
            chunk,
        )
        columns.append(exchange(mixed))
    weights = prepared(
        vertical_standardize_factor,
        vertical_probe_lookup,
        vertical_content_switch,
        vertical_sigmoid_shift,
    ) + (vertical_final_matrix,)
    span = count // parts // COL_CHUNKS
    back = []
    for c in range(COL_CHUNKS):
        back.append(exchange(column_attention(columns, weights, heads, c * span, span)))
    return assemble(back)


def solution(mesh):
    placed = (P("seq", "res", None), P(None, "res", "seq")) + (P(),) * 11
    return jax.shard_map(
        shards, mesh=mesh, in_specs=placed, out_specs=P("seq", "res", None), check_vma=False
    )
```

```python
import functools
import math

import jax
import jax.numpy as jnp
from jax import lax
from jax.experimental import pallas as pl
from jax.experimental.pallas import tpu as pltpu
from jax.sharding import PartitionSpec as P

EPS = 1e-05
LOG2E = math.log2(math.e)
BF, F32 = jnp.bfloat16, jnp.float32
NN = (((1,), (0,)), ((), ()))
NT = (((1,), (1,)), ((), ()))
TN = (((0,), (0,)), ((), ()))
LANES = 128
ONES = 16
KEY_CHUNK = 512
ROW_CHUNKS = 2
COL_CHUNKS = 2


def dot(a, b, dims=NN):
    return lax.dot_general(a, b, dims, preferred_element_type=F32)


def params(limit=None):
    return pltpu.CompilerParams(dimension_semantics=("arbitrary",), vmem_limit_bytes=limit)


def cost(flops, nbytes):
    return pl.CostEstimate(flops=int(flops), bytes_accessed=int(nbytes), transcendentals=0)


def standardize(rows, gain):
    centred = rows - jnp.mean(rows, -1, keepdims=True)
    deviation = jnp.mean(centred * centred, -1, keepdims=True)
    return centred * lax.rsqrt(deviation + EPS) * gain


def whole(array):
    return pl.BlockSpec(
        array.shape, lambda *_: (0,) * array.ndim, pipeline_mode=pl.Buffered(1)
    )


def head_mask(tile, place, size):
    owner = lax.broadcasted_iota(jnp.int32, (tile.shape[0], 1), 0) // size
    return jnp.where(owner == place, tile, jnp.zeros_like(tile))


def project_kernel(size, own, x_ref, gain, wk, wv_t, wq_t, wg_t, shift, k_out, v_out, *rest):
    members, count, features = x_ref.shape
    rows = x_ref[...].astype(F32).reshape(members * count, features)
    normed = standardize(rows, gain[...]).astype(BF)
    k_out[...] = dot(normed, wk[...]).astype(BF).reshape(k_out.shape)
    values = dot(wv_t[...], normed, NT).astype(BF)
    heads, depth = v_out.shape[1:3]
    ones = jnp.ones((depth - size, count), BF)
    if own:
        q_out, g_out = rest
        queries = (dot(wq_t[...], normed, NT) * (LOG2E / math.sqrt(size))).astype(BF)
        gates = jax.nn.sigmoid(dot(wg_t[...], normed, NT) + shift[...])
    for s in range(members):
        at = slice(s * count, (s + 1) * count)
        for h in range(heads):
            v_out[s, h, :size] = values[h * size : (h + 1) * size, at]
            v_out[s, h, size:] = ones
        if own:
            q_out[s] = queries[:, at]
            g_out[s] = gates[:, at]


def project(x, weights, heads, own):
    members, count, features = x.shape
    width = weights[1].shape[1]
    size = width // heads
    rows = size + ONES
    step = math.gcd(members, 4)
    pick3 = lambda s: (s, 0, 0)
    out = [
        jax.ShapeDtypeStruct((members, count, width), BF),
        jax.ShapeDtypeStruct((members, heads, rows, count), BF),
    ]
    specs = [
        pl.BlockSpec((step, count, width), pick3),
        pl.BlockSpec((step, heads, rows, count), lambda s: (s, 0, 0, 0)),
    ]
    if own:
        out += [
            jax.ShapeDtypeStruct((members, width, count), BF),
            jax.ShapeDtypeStruct((members, width, count), F32),
        ]
        specs += [pl.BlockSpec((step, width, count), pick3)] * 2
    return pl.pallas_call(
        functools.partial(project_kernel, size, own),
        grid=(members // step,),
        in_specs=[pl.BlockSpec((step, count, features), pick3)] + [whole(w) for w in weights],
        out_specs=specs,
        out_shape=out,
        compiler_params=params(60 << 20),
        cost_estimate=cost(2 * x.size * width * (4 if own else 2), x.size * 8),
        name="project_own" if own else "project",
    )(x, *weights)


def row_kernel(blocks, parts, size, place, factor, *refs):
    x_ref, q_ref, g_ref, wo = refs[:4]
    keys = refs[4 : 4 + blocks]
    values = refs[4 + blocks : 4 + 2 * blocks]
    priors = refs[4 + 2 * blocks : 4 + 2 * blocks + parts]
    out, bias_s, score_s = refs[4 + 2 * blocks + parts :]
    heads, count, width = bias_s.shape
    block = keys[0].shape[1]
    piece = count // parts

    @pl.when(pl.program_id(0) == 0)
    def _():
        for p in range(parts):
            rows = pl.ds(pl.multiple_of(place[p] * piece, piece), piece)
            for h in range(heads):
                bias_s[h, rows, :] = priors[p][h].astype(F32) * (factor[h] * LOG2E)

    per = LANES // size
    chunk = min(KEY_CHUNK, count)
    each = min(chunk, block)
    attended, top, queries = [], None, None
    for h in range(heads + 1):
        total, high = None, None
        if h < heads:
            group = slice(h // per * LANES, (h // per + 1) * LANES)
            queries = head_mask(q_ref[0, group, :], h % per, size)
        for c in range(count // chunk):
            rows = slice(c * chunk, (c + 1) * chunk)
            places = [divmod(c * chunk + e, block) for e in range(0, chunk, each)]
            if h < heads:
                part = jnp.concatenate([keys[b][0, o : o + each, group] for b, o in places], 0)
                scores = dot(part, queries) + bias_s[h, rows, :]
                score_s[h % 2, rows, :] = scores
                best = jnp.max(scores.reshape(chunk // 8, 8, width), axis=0)
                high = best if high is None else jnp.maximum(high, best)
            if h > 0:
                weights = jnp.exp2(score_s[(h - 1) % 2, rows, :] - top).astype(BF)
                part = jnp.concatenate([values[b][0, h - 1, :, o : o + each] for b, o in places], 1)
                term = dot(part, weights)
                total = term if total is None else total + term
        if h > 0:
            gate = g_ref[0, (h - 1) * size : h * size, :]
            attended.append((total[:size] / total[size : size + 1] * gate).astype(BF))
        if h < heads:
            top = jnp.max(high, axis=0, keepdims=True)
    joined = jnp.concatenate(attended, 0)
    mixed = x_ref[0].astype(F32) + dot(joined, wo[...], TN)
    out[:, 0] = mixed.astype(BF).reshape(parts, out.shape[2], mixed.shape[1])


def row_attention(place, factor, x, q, g, wo, keys, values, priors, first, members):
    blocks, parts = len(keys), len(priors)
    heads = factor.shape[0]
    _, count, features = x.shape
    width = q.shape[1]
    size = width // heads
    total = blocks * count
    pick3 = lambda s, *_: (first + s, 0, 0)
    pick4 = lambda s, *_: (first + s, 0, 0, 0)
    sub = count // parts
    grid_spec = pltpu.PrefetchScalarGridSpec(
        num_scalar_prefetch=2,
        grid=(members,),
        in_specs=[
            pl.BlockSpec((1, count, features), pick3),
            pl.BlockSpec((1, width, count), pick3),
            pl.BlockSpec((1, width, count), pick3),
            whole(wo),
        ]
        + [pl.BlockSpec((1,) + k.shape[1:], pick3) for k in keys]
        + [pl.BlockSpec((1,) + v.shape[1:], pick4) for v in values]
        + [whole(b) for b in priors],
        out_specs=pl.BlockSpec((parts, 1, sub, features), lambda s, *_: (0, s, 0, 0)),
        scratch_shapes=[
            pltpu.VMEM((heads, total, count), F32),
            pltpu.VMEM((2, total, count), F32),
        ],
    )
    work = 2 * members * total * count * width * 16
    return pl.pallas_call(
        functools.partial(row_kernel, blocks, parts, size),
        grid_spec=grid_spec,
        out_shape=jax.ShapeDtypeStruct((parts, members, sub, features), BF),
        compiler_params=params(60 << 20),
        cost_estimate=cost(work, priors[0].size * parts * 2),
        name="row_attention",
    )(place, factor, x, q, g, wo, *keys, *values, *priors)


def column_kernel(chunks, heads, *refs):
    xs = refs[:chunks]
    gain, wk, wv_t, wq_t, wg_t, shift, wo = refs[chunks : chunks + 7]
    out, x_s, n_s, o_s = refs[chunks + 7 :]
    parts, members, residues, features = xs[0].shape
    slots = parts * chunks
    width = wk.shape[1]
    size = width // heads
    each = members * residues
    rows = slots * each
    seqs = slots * members
    for k in range(slots):
        block = xs[k % chunks][k // chunks].astype(F32)
        x_s[k * each : (k + 1) * each, :] = block.reshape(each, features)
    normed = standardize(x_s[...], gain[...])
    tiles = range(features // LANES)
    for i in tiles:
        n_s[i] = normed[:, i * LANES : (i + 1) * LANES]

    def strided(ref, r):
        return jnp.concatenate([ref[i, pl.ds(r, seqs, stride=residues), :] for i in tiles], 1)

    normed = jnp.concatenate([strided(n_s, r).astype(BF) for r in range(residues)], 0)
    scale = LOG2E / math.sqrt(size)
    keys = dot(normed, wk[...]).astype(BF)
    values = dot(wv_t[...], normed, NT).astype(BF)
    queries = (dot(wq_t[...], normed, NT) * scale).astype(BF)
    gates = jax.nn.sigmoid(dot(wg_t[...], normed, NT) + shift[...])
    join = max(1, LANES // seqs)
    span = join * seqs
    per = LANES // size
    ones = jnp.ones((ONES, span), BF)
    lane = lax.broadcasted_iota(jnp.int32, (1, span), 1) // seqs
    for t in range(residues // join):
        cols = slice(t * span, (t + 1) * span)
        attended = []
        crosses = []
        for h in range(heads):
            group = slice(h // per * LANES, (h // per + 1) * LANES)
            crosses.append(dot(keys[cols, group], head_mask(queries[group, cols], h % per, size)))
        spreads = []
        for crossed in crosses:
            scores = crossed[:seqs]
            for i in range(1, join):
                scores = jnp.where(lane == i, crossed[i * seqs : (i + 1) * seqs], scores)
            weights = jnp.exp2(scores - jnp.max(scores, axis=0, keepdims=True)).astype(BF)
            spread = [jnp.where(lane == i, weights, jnp.zeros_like(weights)) for i in range(join)]
            spreads.append(jnp.concatenate(spread, 0))
        for h, spread in enumerate(spreads):
            part = jnp.concatenate([values[h * size : (h + 1) * size, cols], ones], 0)
            total = dot(part, spread)
            gate = gates[h * size : (h + 1) * size, cols]
            attended.append((total[:size] / total[size : size + 1] * gate).astype(BF))
        update = dot(jnp.concatenate(attended, 0), wo[...], TN)
        for i in range(join):
            pick = pl.ds(t * join + i, seqs, stride=residues)
            for j in tiles:
                part = update[i * seqs : (i + 1) * seqs, j * LANES : (j + 1) * LANES]
                o_s[j, pick, :] = part
    for k in range(slots):
        at = slice(k * each, (k + 1) * each)
        rows = x_s[at, :] + jnp.concatenate([o_s[j, at, :] for j in tiles], 1)
        at = slice(k % chunks * members, (k % chunks + 1) * members)
        out[k // chunks, at] = rows.astype(BF).reshape(members, residues, features)


def column_attention(xs, weights, heads, first, residues):
    chunks = len(xs)
    parts, members, _, features = xs[0].shape
    step = 8
    rows = parts * chunks * members * step
    offset = first // step
    return pl.pallas_call(
        functools.partial(column_kernel, chunks, heads),
        grid=(residues // step,),
        in_specs=[
            pl.BlockSpec((parts, members, step, features), lambda r: (0, 0, offset + r, 0))
        ]
        * chunks
        + [whole(w) for w in weights],
        out_specs=pl.BlockSpec(
            (parts, members * chunks, step, features), lambda r: (0, 0, r, 0)
        ),
        out_shape=jax.ShapeDtypeStruct((parts, members * chunks, residues, features), BF),
        scratch_shapes=[pltpu.VMEM((rows, features), F32)]
        + [pltpu.VMEM((features // LANES, rows, LANES), F32)] * 2,
        compiler_params=params(60 << 20),
        cost_estimate=cost(2 * rows // step * residues * features * features * 30, rows * 8),
        name="column_attention",
    )(*xs, *weights)


def assemble_kernel(block, *refs):
    out = refs[-1]
    for k in range(block.shape[0]):
        out[:, k, 0] = block[k].astype(F32)


def assemble(block, c, chunks, earlier):
    parts, members, rows, features = block.shape
    step = math.gcd(members, 4)
    shape = (members, parts, chunks, rows, features)
    held = [] if earlier is None else [earlier]
    return pl.pallas_call(
        assemble_kernel,
        grid=(members // step,),
        in_specs=[pl.BlockSpec((parts, step, rows, features), lambda s: (0, s, 0, 0))]
        + [pl.BlockSpec(memory_space=pl.ANY)] * len(held),
        out_specs=pl.BlockSpec((step, parts, 1, rows, features), lambda s: (s, 0, c, 0, 0)),
        out_shape=jax.ShapeDtypeStruct(shape, F32),
        input_output_aliases={1: 0} if held else {},
        compiler_params=params(),
        cost_estimate=cost(0, block.size * 6),
        name="assemble",
    )(block, *held)


def shards(
    alignment_embedding,
    unscaled_edge_prior,
    edge_prior_factor,
    horizontal_standardize_factor,
    horizontal_probe_lookup,
    horizontal_content_switch,
    horizontal_sigmoid_shift,
    horizontal_final_matrix,
    vertical_standardize_factor,
    vertical_probe_lookup,
    vertical_content_switch,
    vertical_sigmoid_shift,
    vertical_final_matrix,
):
    x = alignment_embedding
    members, count, features = x.shape
    heads = edge_prior_factor.shape[0]
    parts, blocks = lax.axis_size("seq"), lax.axis_size("res")
    seq, res = lax.axis_index("seq"), lax.axis_index("res")
    piece = unscaled_edge_prior.shape[2]

    def swap(array, axis, size, bits):
        return lax.ppermute(array, axis, [(i, i ^ bits) for i in range(size)])

    prior = jnp.swapaxes(unscaled_edge_prior, 1, 2)
    doubled = {0: prior}
    top = parts.bit_length() - 1
    first = swap(prior, "seq", parts, 1 << (top - 1))
    for b in reversed(range(1, top)):
        step = 1 << b
        for m in [m for m in doubled]:
            doubled[m ^ step] = first if b == top - 1 else swap(doubled[m], "seq", parts, step)
    near = [swap(x, "res", blocks, 1 << b) for b in range(blocks.bit_length() - 1)]
    order = sorted(doubled)
    order = order + [m ^ 1 for m in order]
    owners = jnp.stack([seq ^ m for m in order])
    per = count // piece
    place = ((owners // per) ^ res) * per + owners % per

    def prepared(gain, probe, switch, offset):
        return (
            gain[None],
            probe[1],
            switch[0].T,
            probe[0].T,
            switch[1].T,
            offset[:, None],
        )

    weights = prepared(
        horizontal_standardize_factor,
        horizontal_probe_lookup,
        horizontal_content_switch,
        horizontal_sigmoid_shift,
    )
    keys, values = [None] * blocks, [None] * blocks
    keys[0], values[0], queries, gates = project(x, weights, heads, True)
    half = members // 2
    if blocks == 4:
        far = [
            swap(near[0][:half], "res", blocks, 2),
            swap(near[1][half:], "res", blocks, 1),
        ]
        x_slots = [x, near[0], near[1], jnp.concatenate(far, 0)]
    else:
        bits = {1 << b: rows for b, rows in enumerate(near)}
        x_slots = [x] + [
            bits[m] if m in bits else swap(x, "res", blocks, m) for m in range(1, blocks)
        ]
    for m in range(1, blocks):
        keys[m], values[m] = project(x_slots[m], weights, heads, False)
    priors = [doubled[m] for m in sorted(doubled)]
    last, keys = lax.optimization_barrier((priors[-1], keys))
    priors[-1] = last
    priors = priors + [swap(p, "seq", parts, 1) for p in priors]
    place = place.astype(jnp.int32)
    exchange = functools.partial(
        lax.all_to_all, axis_name="seq", split_axis=0, concat_axis=0, tiled=True
    )
    columns = []
    chunk = members // ROW_CHUNKS
    for c in range(ROW_CHUNKS):
        mixed = row_attention(
            place,
            edge_prior_factor,
            x,
            queries,
            gates,
            horizontal_final_matrix,
            keys,
            values,
            priors,
            c * chunk,
            chunk,
        )
        columns.append(exchange(mixed))
    weights = prepared(
        vertical_standardize_factor,
        vertical_probe_lookup,
        vertical_content_switch,
        vertical_sigmoid_shift,
    ) + (vertical_final_matrix,)
    span = count // parts // COL_CHUNKS
    back = []
    for c in range(COL_CHUNKS):
        back.append(exchange(column_attention(columns, weights, heads, c * span, span)))
    out = None
    for c in range(COL_CHUNKS):
        out = assemble(back[c], c, COL_CHUNKS, out)
    return out.reshape(members, count, features)


def solution(mesh):
    placed = (P("seq", "res", None), P(None, "res", "seq")) + (P(),) * 11
    return jax.shard_map(
        shards, mesh=mesh, in_specs=placed, out_specs=P("seq", "res", None), check_vma=False
    )
```

```python
import functools
import math

import jax
import jax.numpy as jnp
from jax import lax
from jax.experimental import pallas as pl
from jax.experimental.pallas import tpu as pltpu
from jax.sharding import PartitionSpec as P

EPS = 1e-05
LOG2E = math.log2(math.e)
BF, F32 = jnp.bfloat16, jnp.float32
NN = (((1,), (0,)), ((), ()))
NT = (((1,), (1,)), ((), ()))
TN = (((0,), (0,)), ((), ()))
LANES = 128
ONES = 16
KEY_CHUNK = 512
ROW_CHUNKS = 2
COL_CHUNKS = 2


def dot(a, b, dims=NN):
    return lax.dot_general(a, b, dims, preferred_element_type=F32)


def params(limit=None):
    return pltpu.CompilerParams(dimension_semantics=("arbitrary",), vmem_limit_bytes=limit)


def cost(flops, nbytes):
    return pl.CostEstimate(flops=int(flops), bytes_accessed=int(nbytes), transcendentals=0)


def standardize(rows, gain):
    centred = rows - jnp.mean(rows, -1, keepdims=True)
    deviation = jnp.mean(centred * centred, -1, keepdims=True)
    return centred * lax.rsqrt(deviation + EPS) * gain


def whole(array):
    return pl.BlockSpec(
        array.shape, lambda *_: (0,) * array.ndim, pipeline_mode=pl.Buffered(1)
    )


def head_mask(tile, place, size):
    owner = lax.broadcasted_iota(jnp.int32, (tile.shape[0], 1), 0) // size
    return jnp.where(owner == place, tile, jnp.zeros_like(tile))


def project_kernel(size, own, x_ref, gain, wk, wv_t, wq_t, wg_t, shift, k_out, v_out, *rest):
    members, count, features = x_ref.shape
    rows = x_ref[...].astype(F32).reshape(members * count, features)
    normed = standardize(rows, gain[...]).astype(BF)
    k_out[...] = dot(normed, wk[...]).astype(BF).reshape(k_out.shape)
    values = dot(wv_t[...], normed, NT).astype(BF)
    heads, depth = v_out.shape[1:3]
    ones = jnp.ones((depth - size, count), BF)
    if own:
        q_out, g_out = rest
        queries = (dot(wq_t[...], normed, NT) * (LOG2E / math.sqrt(size))).astype(BF)
        gates = jax.nn.sigmoid(dot(wg_t[...], normed, NT) + shift[...])
    for s in range(members):
        at = slice(s * count, (s + 1) * count)
        for h in range(heads):
            v_out[s, h, :size] = values[h * size : (h + 1) * size, at]
            v_out[s, h, size:] = ones
        if own:
            q_out[s] = queries[:, at]
            g_out[s] = gates[:, at]


def project(x, weights, heads, own):
    members, count, features = x.shape
    width = weights[1].shape[1]
    size = width // heads
    rows = size + ONES
    step = math.gcd(members, 4)
    pick3 = lambda s: (s, 0, 0)
    out = [
        jax.ShapeDtypeStruct((members, count, width), BF),
        jax.ShapeDtypeStruct((members, heads, rows, count), BF),
    ]
    specs = [
        pl.BlockSpec((step, count, width), pick3),
        pl.BlockSpec((step, heads, rows, count), lambda s: (s, 0, 0, 0)),
    ]
    if own:
        out += [
            jax.ShapeDtypeStruct((members, width, count), BF),
            jax.ShapeDtypeStruct((members, width, count), F32),
        ]
        specs += [pl.BlockSpec((step, width, count), pick3)] * 2
    return pl.pallas_call(
        functools.partial(project_kernel, size, own),
        grid=(members // step,),
        in_specs=[pl.BlockSpec((step, count, features), pick3)] + [whole(w) for w in weights],
        out_specs=specs,
        out_shape=out,
        compiler_params=params(24 << 20),
        cost_estimate=cost(2 * x.size * width * (4 if own else 2), x.size * 8),
        name="project_own" if own else "project",
    )(x, *weights)


def row_kernel(blocks, parts, size, place, factor, *refs):
    x_ref, q_ref, g_ref, wo = refs[:4]
    keys = refs[4 : 4 + blocks]
    values = refs[4 + blocks : 4 + 2 * blocks]
    priors = refs[4 + 2 * blocks : 4 + 2 * blocks + parts]
    out, bias_s, score_s = refs[4 + 2 * blocks + parts :]
    heads, count, width = bias_s.shape
    block = keys[0].shape[1]
    piece = count // parts

    @pl.when(pl.program_id(0) == 0)
    def _():
        for p in range(parts):
            rows = pl.ds(pl.multiple_of(place[p] * piece, piece), piece)
            for h in range(heads):
                bias_s[h, rows, :] = priors[p][h].astype(F32) * (factor[h] * LOG2E)

    per = LANES // size
    chunk = min(KEY_CHUNK, count)
    each = min(chunk, block)
    attended, top, queries = [], None, None
    for h in range(heads + 1):
        total, high = None, None
        if h < heads:
            group = slice(h // per * LANES, (h // per + 1) * LANES)
            queries = head_mask(q_ref[0, group, :], h % per, size)
        for c in range(count // chunk):
            rows = slice(c * chunk, (c + 1) * chunk)
            places = [divmod(c * chunk + e, block) for e in range(0, chunk, each)]
            if h < heads:
                part = jnp.concatenate([keys[b][0, o : o + each, group] for b, o in places], 0)
                scores = dot(part, queries) + bias_s[h, rows, :]
                score_s[h % 2, rows, :] = scores
                best = jnp.max(scores.reshape(chunk // 8, 8, width), axis=0)
                high = best if high is None else jnp.maximum(high, best)
            if h > 0:
                weights = jnp.exp2(score_s[(h - 1) % 2, rows, :] - top).astype(BF)
                part = jnp.concatenate([values[b][0, h - 1, :, o : o + each] for b, o in places], 1)
                term = dot(part, weights)
                total = term if total is None else total + term
        if h > 0:
            gate = g_ref[0, (h - 1) * size : h * size, :]
            attended.append((total[:size] / total[size : size + 1] * gate).astype(BF))
        if h < heads:
            top = jnp.max(high, axis=0, keepdims=True)
    joined = jnp.concatenate(attended, 0)
    mixed = x_ref[0].astype(F32) + dot(joined, wo[...], TN)
    out[:, 0] = mixed.astype(BF).reshape(parts, out.shape[2], mixed.shape[1])


def row_attention(place, factor, x, q, g, wo, keys, values, priors, first, members):
    blocks, parts = len(keys), len(priors)
    heads = factor.shape[0]
    _, count, features = x.shape
    width = q.shape[1]
    size = width // heads
    total = blocks * count
    pick3 = lambda s, *_: (first + s, 0, 0)
    pick4 = lambda s, *_: (first + s, 0, 0, 0)
    sub = count // parts
    grid_spec = pltpu.PrefetchScalarGridSpec(
        num_scalar_prefetch=2,
        grid=(members,),
        in_specs=[
            pl.BlockSpec((1, count, features), pick3),
            pl.BlockSpec((1, width, count), pick3),
            pl.BlockSpec((1, width, count), pick3),
            whole(wo),
        ]
        + [pl.BlockSpec((1,) + k.shape[1:], pick3) for k in keys]
        + [pl.BlockSpec((1,) + v.shape[1:], pick4) for v in values]
        + [whole(b) for b in priors],
        out_specs=pl.BlockSpec((parts, 1, sub, features), lambda s, *_: (0, s, 0, 0)),
        scratch_shapes=[
            pltpu.VMEM((heads, total, count), F32),
            pltpu.VMEM((2, total, count), F32),
        ],
    )
    far = lambda array: pltpu.with_memory_space_constraint(array, pltpu.HBM)
    streamed, rest = [far(a) for a in (x, q, g)], [far(a) for a in (*keys, *values)]
    work = 2 * members * total * count * width * 16
    held = 4 * heads * total * count + 8 * total * count + 2 * priors[0].size * parts
    moved = 2 * (sum(a.size // a.shape[0] for a in (*keys, *values)) * 2 + 8 * width * count)
    limit = (held + moved) * 5 // 4 + (4 << 20)
    return pl.pallas_call(
        functools.partial(row_kernel, blocks, parts, size),
        grid_spec=grid_spec,
        out_shape=jax.ShapeDtypeStruct((parts, members, sub, features), BF),
        compiler_params=params(limit),
        cost_estimate=cost(work, priors[0].size * parts * 2),
        name="row_attention",
    )(place, factor, *streamed, wo, *rest, *priors)


def column_kernel(chunks, heads, *refs):
    xs = refs[:chunks]
    gain, wk, wv_t, wq_t, wg_t, shift, wo = refs[chunks : chunks + 7]
    out, x_s, n_s, o_s = refs[chunks + 7 :]
    parts, members, residues, features = xs[0].shape
    slots = parts * chunks
    width = wk.shape[1]
    size = width // heads
    each = members * residues
    rows = slots * each
    seqs = slots * members
    for k in range(slots):
        block = xs[k % chunks][k // chunks].astype(F32)
        x_s[k * each : (k + 1) * each, :] = block.reshape(each, features)
    normed = standardize(x_s[...], gain[...])
    tiles = range(features // LANES)
    for i in tiles:
        n_s[i] = normed[:, i * LANES : (i + 1) * LANES]

    def strided(ref, r):
        return jnp.concatenate([ref[i, pl.ds(r, seqs, stride=residues), :] for i in tiles], 1)

    normed = jnp.concatenate([strided(n_s, r).astype(BF) for r in range(residues)], 0)
    scale = LOG2E / math.sqrt(size)
    keys = dot(normed, wk[...]).astype(BF)
    values = dot(wv_t[...], normed, NT).astype(BF)
    queries = (dot(wq_t[...], normed, NT) * scale).astype(BF)
    gates = jax.nn.sigmoid(dot(wg_t[...], normed, NT) + shift[...])
    join = max(1, LANES // seqs)
    span = join * seqs
    per = LANES // size
    ones = jnp.ones((ONES, span), BF)
    lane = lax.broadcasted_iota(jnp.int32, (1, span), 1) // seqs
    for t in range(residues // join):
        cols = slice(t * span, (t + 1) * span)
        attended = []
        crosses = []
        for h in range(heads):
            group = slice(h // per * LANES, (h // per + 1) * LANES)
            crosses.append(dot(keys[cols, group], head_mask(queries[group, cols], h % per, size)))
        spreads = []
        for crossed in crosses:
            scores = crossed[:seqs]
            for i in range(1, join):
                scores = jnp.where(lane == i, crossed[i * seqs : (i + 1) * seqs], scores)
            weights = jnp.exp2(scores - jnp.max(scores, axis=0, keepdims=True)).astype(BF)
            spread = [jnp.where(lane == i, weights, jnp.zeros_like(weights)) for i in range(join)]
            spreads.append(jnp.concatenate(spread, 0))
        for h, spread in enumerate(spreads):
            part = jnp.concatenate([values[h * size : (h + 1) * size, cols], ones], 0)
            total = dot(part, spread)
            gate = gates[h * size : (h + 1) * size, cols]
            attended.append((total[:size] / total[size : size + 1] * gate).astype(BF))
        update = dot(jnp.concatenate(attended, 0), wo[...], TN)
        for i in range(join):
            pick = pl.ds(t * join + i, seqs, stride=residues)
            for j in tiles:
                part = update[i * seqs : (i + 1) * seqs, j * LANES : (j + 1) * LANES]
                o_s[j, pick, :] = part
    for k in range(slots):
        at = slice(k * each, (k + 1) * each)
        rows = x_s[at, :] + jnp.concatenate([o_s[j, at, :] for j in tiles], 1)
        at = slice(k % chunks * members, (k % chunks + 1) * members)
        out[k // chunks, at] = rows.astype(BF).reshape(members, residues, features)


def column_attention(xs, weights, heads, first, residues):
    chunks = len(xs)
    parts, members, _, features = xs[0].shape
    step = 8
    rows = parts * chunks * members * step
    offset = first // step
    return pl.pallas_call(
        functools.partial(column_kernel, chunks, heads),
        grid=(residues // step,),
        in_specs=[
            pl.BlockSpec((parts, members, step, features), lambda r: (0, 0, offset + r, 0))
        ]
        * chunks
        + [whole(w) for w in weights],
        out_specs=pl.BlockSpec(
            (parts, members * chunks, step, features), lambda r: (0, 0, r, 0)
        ),
        out_shape=jax.ShapeDtypeStruct((parts, members * chunks, residues, features), BF),
        scratch_shapes=[pltpu.VMEM((rows, features), F32)]
        + [pltpu.VMEM((features // LANES, rows, LANES), F32)] * 2,
        compiler_params=params(24 << 20),
        cost_estimate=cost(2 * rows // step * residues * features * features * 30, rows * 8),
        name="column_attention",
    )(*xs, *weights)


def assemble_kernel(block, *refs):
    out = refs[-1]
    for k in range(block.shape[0]):
        out[:, k, 0] = block[k].astype(F32)


def assemble(block, c, chunks, earlier):
    parts, members, rows, features = block.shape
    step = math.gcd(members, 4)
    shape = (members, parts, chunks, rows, features)
    held = [] if earlier is None else [earlier]
    return pl.pallas_call(
        assemble_kernel,
        grid=(members // step,),
        in_specs=[pl.BlockSpec((parts, step, rows, features), lambda s: (0, s, 0, 0))]
        + [pl.BlockSpec(memory_space=pl.ANY)] * len(held),
        out_specs=pl.BlockSpec((step, parts, 1, rows, features), lambda s: (s, 0, c, 0, 0)),
        out_shape=jax.ShapeDtypeStruct(shape, F32),
        input_output_aliases={1: 0} if held else {},
        compiler_params=params(16 << 20),
        cost_estimate=cost(0, block.size * 6),
        name="assemble",
    )(block, *held)


def shards(
    alignment_embedding,
    unscaled_edge_prior,
    edge_prior_factor,
    horizontal_standardize_factor,
    horizontal_probe_lookup,
    horizontal_content_switch,
    horizontal_sigmoid_shift,
    horizontal_final_matrix,
    vertical_standardize_factor,
    vertical_probe_lookup,
    vertical_content_switch,
    vertical_sigmoid_shift,
    vertical_final_matrix,
):
    x = alignment_embedding
    members, count, features = x.shape
    heads = edge_prior_factor.shape[0]
    parts, blocks = lax.axis_size("seq"), lax.axis_size("res")
    seq, res = lax.axis_index("seq"), lax.axis_index("res")
    piece = unscaled_edge_prior.shape[2]

    def swap(array, axis, size, bits):
        return lax.ppermute(array, axis, [(i, i ^ bits) for i in range(size)])

    prior = jnp.swapaxes(unscaled_edge_prior, 1, 2)
    doubled = {0: prior}
    top = parts.bit_length() - 1
    first = swap(prior, "seq", parts, 1 << (top - 1))
    for b in reversed(range(1, top)):
        step = 1 << b
        for m in [m for m in doubled]:
            doubled[m ^ step] = first if b == top - 1 else swap(doubled[m], "seq", parts, step)
    near = [swap(x, "res", blocks, 1 << b) for b in range(blocks.bit_length() - 1)]
    order = sorted(doubled)
    order = order + [m ^ 1 for m in order]
    owners = jnp.stack([seq ^ m for m in order])
    per = count // piece
    place = ((owners // per) ^ res) * per + owners % per

    def prepared(gain, probe, switch, offset):
        return (
            gain[None],
            probe[1],
            switch[0].T,
            probe[0].T,
            switch[1].T,
            offset[:, None],
        )

    weights = prepared(
        horizontal_standardize_factor,
        horizontal_probe_lookup,
        horizontal_content_switch,
        horizontal_sigmoid_shift,
    )
    keys, values = [None] * blocks, [None] * blocks
    keys[0], values[0], queries, gates = project(x, weights, heads, True)
    near, queries = lax.optimization_barrier((near, queries))
    half = members // 2
    if blocks == 4:
        far = [
            swap(near[0][:half], "res", blocks, 2),
            swap(near[1][half:], "res", blocks, 1),
        ]
        x_slots = [x, near[0], near[1], jnp.concatenate(far, 0)]
    else:
        bits = {1 << b: rows for b, rows in enumerate(near)}
        x_slots = [x] + [
            bits[m] if m in bits else swap(x, "res", blocks, m) for m in range(1, blocks)
        ]
    for m in range(1, blocks):
        keys[m], values[m] = project(x_slots[m], weights, heads, False)
    priors = [doubled[m] for m in sorted(doubled)]
    last, keys = lax.optimization_barrier((priors[-1], keys))
    priors[-1] = last
    priors = priors + [swap(p, "seq", parts, 1) for p in priors]
    place = place.astype(jnp.int32)
    exchange = functools.partial(
        lax.all_to_all, axis_name="seq", split_axis=0, concat_axis=0, tiled=True
    )
    columns = []
    chunk = members // ROW_CHUNKS
    for c in range(ROW_CHUNKS):
        mixed = row_attention(
            place,
            edge_prior_factor,
            x,
            queries,
            gates,
            horizontal_final_matrix,
            keys,
            values,
            priors,
            c * chunk,
            chunk,
        )
        columns.append(exchange(mixed))
    weights = prepared(
        vertical_standardize_factor,
        vertical_probe_lookup,
        vertical_content_switch,
        vertical_sigmoid_shift,
    ) + (vertical_final_matrix,)
    span = count // parts // COL_CHUNKS
    back = []
    for c in range(COL_CHUNKS):
        back.append(exchange(column_attention(columns, weights, heads, c * span, span)))
    out = None
    for c in range(COL_CHUNKS):
        out = assemble(back[c], c, COL_CHUNKS, out)
    return out.reshape(members, count, features)


def solution(mesh):
    placed = (P("seq", "res", None), P(None, "res", "seq")) + (P(),) * 11
    return jax.shard_map(
        shards, mesh=mesh, in_specs=placed, out_specs=P("seq", "res", None), check_vma=False
    )
```

```python
import functools
import math

import jax
import jax.numpy as jnp
from jax import lax
from jax.experimental import pallas as pl
from jax.experimental.pallas import tpu as pltpu
from jax.sharding import PartitionSpec as P

EPS = 1e-05
LOG2E = math.log2(math.e)
BF, F32 = jnp.bfloat16, jnp.float32
NN = (((1,), (0,)), ((), ()))
NT = (((1,), (1,)), ((), ()))
TN = (((0,), (0,)), ((), ()))
LANES = 128
ONES = 16
KEY_CHUNK = 512
ROW_CHUNKS = 2
COL_CHUNKS = 2


def dot(a, b, dims=NN):
    return lax.dot_general(a, b, dims, preferred_element_type=F32)


def params(limit=None):
    return pltpu.CompilerParams(dimension_semantics=("arbitrary",), vmem_limit_bytes=limit)


def cost(flops, nbytes):
    return pl.CostEstimate(flops=int(flops), bytes_accessed=int(nbytes), transcendentals=0)


def standardize(rows, gain):
    centred = rows - jnp.mean(rows, -1, keepdims=True)
    deviation = jnp.mean(centred * centred, -1, keepdims=True)
    return centred * lax.rsqrt(deviation + EPS) * gain


def whole(array):
    return pl.BlockSpec(
        array.shape, lambda *_: (0,) * array.ndim, pipeline_mode=pl.Buffered(1)
    )


def head_mask(tile, place, size):
    owner = lax.broadcasted_iota(jnp.int32, (tile.shape[0], 1), 0) // size
    return jnp.where(owner == place, tile, jnp.zeros_like(tile))


def project_kernel(size, own, x_ref, gain, wk, wv_t, wq_t, wg_t, shift, k_out, v_out, *rest):
    members, count, features = x_ref.shape
    rows = x_ref[...].astype(F32).reshape(members * count, features)
    normed = standardize(rows, gain[...]).astype(BF)
    k_out[...] = dot(normed, wk[...]).astype(BF).reshape(k_out.shape)
    values = dot(wv_t[...], normed, NT).astype(BF)
    heads, depth = v_out.shape[1:3]
    ones = jnp.ones((depth - size, count), BF)
    if own:
        q_out, g_out = rest
        queries = (dot(wq_t[...], normed, NT) * (LOG2E / math.sqrt(size))).astype(BF)
        gates = jax.nn.sigmoid(dot(wg_t[...], normed, NT) + shift[...])
    for s in range(members):
        at = slice(s * count, (s + 1) * count)
        for h in range(heads):
            v_out[s, h, :size] = values[h * size : (h + 1) * size, at]
            v_out[s, h, size:] = ones
        if own:
            q_out[s] = queries[:, at]
            g_out[s] = gates[:, at]


def project(x, weights, heads, own):
    members, count, features = x.shape
    width = weights[1].shape[1]
    size = width // heads
    rows = size + ONES
    step = math.gcd(members, 4)
    pick3 = lambda s: (s, 0, 0)
    out = [
        jax.ShapeDtypeStruct((members, count, width), BF),
        jax.ShapeDtypeStruct((members, heads, rows, count), BF),
    ]
    specs = [
        pl.BlockSpec((step, count, width), pick3),
        pl.BlockSpec((step, heads, rows, count), lambda s: (s, 0, 0, 0)),
    ]
    if own:
        out += [
            jax.ShapeDtypeStruct((members, width, count), BF),
            jax.ShapeDtypeStruct((members, width, count), F32),
        ]
        specs += [pl.BlockSpec((step, width, count), pick3)] * 2
    return pl.pallas_call(
        functools.partial(project_kernel, size, own),
        grid=(members // step,),
        in_specs=[pl.BlockSpec((step, count, features), pick3)] + [whole(w) for w in weights],
        out_specs=specs,
        out_shape=out,
        compiler_params=params(24 << 20),
        cost_estimate=cost(2 * x.size * width * (4 if own else 2), x.size * 8),
        name="project_own" if own else "project",
    )(x, *weights)


def row_kernel(blocks, parts, size, split, place, factor, me, *refs):
    x_ref, q_ref, g_ref, wo = refs[:4]
    keys = refs[4 : 4 + blocks]
    values = refs[4 + blocks : 4 + 2 * blocks]
    priors = refs[4 + 2 * blocks : 4 + 2 * blocks + parts]
    outs = refs[4 + 2 * blocks + parts : -3]
    bias_s, score_s, mixed_s = refs[-3:]
    heads, count, width = bias_s.shape
    block = keys[0].shape[1]
    piece = count // parts

    @pl.when(pl.program_id(0) == 0)
    def _():
        for p in range(parts):
            rows = pl.ds(pl.multiple_of(place[p] * piece, piece), piece)
            for h in range(heads):
                bias_s[h, rows, :] = priors[p][h].astype(F32) * (factor[h] * LOG2E)

    per = LANES // size
    chunk = min(KEY_CHUNK, count)
    each = min(chunk, block)
    attended, top, queries = [], None, None
    for h in range(heads + 1):
        total, high = None, None
        if h < heads:
            group = slice(h // per * LANES, (h // per + 1) * LANES)
            queries = head_mask(q_ref[0, group, :], h % per, size)
        for c in range(count // chunk):
            rows = slice(c * chunk, (c + 1) * chunk)
            places = [divmod(c * chunk + e, block) for e in range(0, chunk, each)]
            if h < heads:
                part = jnp.concatenate([keys[b][0, o : o + each, group] for b, o in places], 0)
                scores = dot(part, queries) + bias_s[h, rows, :]
                score_s[h % 2, rows, :] = scores
                best = jnp.max(scores.reshape(chunk // 8, 8, width), axis=0)
                high = best if high is None else jnp.maximum(high, best)
            if h > 0:
                weights = jnp.exp2(score_s[(h - 1) % 2, rows, :] - top).astype(BF)
                part = jnp.concatenate([values[b][0, h - 1, :, o : o + each] for b, o in places], 1)
                term = dot(part, weights)
                total = term if total is None else total + term
        if h > 0:
            gate = g_ref[0, (h - 1) * size : h * size, :]
            attended.append((total[:size] / total[size : size + 1] * gate).astype(BF))
        if h < heads:
            top = jnp.max(high, axis=0, keepdims=True)
    joined = jnp.concatenate(attended, 0)
    mixed = x_ref[0].astype(F32) + dot(joined, wo[...], TN)
    if split:
        mixed_s[...] = mixed
        for m in range(parts):
            sub = outs[m].shape[1]
            at = pl.ds(pl.multiple_of((me[0] ^ m) * sub, sub), sub)
            outs[m][0] = mixed_s[at, :].astype(BF)
    else:
        outs[0][:, 0] = mixed.astype(BF).reshape(parts, outs[0].shape[2], mixed.shape[1])


def row_attention(place, factor, me, x, q, g, wo, keys, values, priors, first, members, split):
    blocks, parts = len(keys), len(priors)
    heads = factor.shape[0]
    _, count, features = x.shape
    width = q.shape[1]
    size = width // heads
    total = blocks * count
    pick3 = lambda s, *_: (first + s, 0, 0)
    pick4 = lambda s, *_: (first + s, 0, 0, 0)
    sub = count // parts
    if split:
        out_specs = [pl.BlockSpec((1, sub, features), lambda s, *_: (s, 0, 0))] * parts
        out_shape = [jax.ShapeDtypeStruct((members, sub, features), BF)] * parts
    else:
        out_specs = [pl.BlockSpec((parts, 1, sub, features), lambda s, *_: (0, s, 0, 0))]
        out_shape = [jax.ShapeDtypeStruct((parts, members, sub, features), BF)]
    grid_spec = pltpu.PrefetchScalarGridSpec(
        num_scalar_prefetch=3,
        grid=(members,),
        in_specs=[
            pl.BlockSpec((1, count, features), pick3),
            pl.BlockSpec((1, width, count), pick3),
            pl.BlockSpec((1, width, count), pick3),
            whole(wo),
        ]
        + [pl.BlockSpec((1,) + k.shape[1:], pick3) for k in keys]
        + [pl.BlockSpec((1,) + v.shape[1:], pick4) for v in values]
        + [whole(b) for b in priors],
        out_specs=out_specs,
        scratch_shapes=[
            pltpu.VMEM((heads, total, count), F32),
            pltpu.VMEM((2, total, count), F32),
            pltpu.VMEM((count, features), F32),
        ],
    )
    far = lambda array: pltpu.with_memory_space_constraint(array, pltpu.HBM)
    streamed, rest = [far(a) for a in (x, q, g)], [far(a) for a in (*keys, *values)]
    work = 2 * members * total * count * width * 16
    held = 4 * heads * total * count + 8 * total * count + 2 * priors[0].size * parts
    moved = 2 * (sum(a.size // a.shape[0] for a in (*keys, *values)) * 2 + 8 * width * count)
    limit = (held + moved) * 5 // 4 + (4 << 20)
    return pl.pallas_call(
        functools.partial(row_kernel, blocks, parts, size, split),
        grid_spec=grid_spec,
        out_shape=out_shape,
        compiler_params=params(limit),
        cost_estimate=cost(work, priors[0].size * parts * 2),
        name="row_attention",
    )(place, factor, me, *streamed, wo, *rest, *priors)


def column_kernel(counts, parts, heads, split, me, *refs):
    chunks, given = len(counts), sum(counts)
    xs = refs[:given]
    gain, wk, wv_t, wq_t, wg_t, shift, wo = refs[given : given + 7]
    outs = refs[given + 7 : -3]
    x_s, n_s, o_s = refs[-3:]
    members, residues, features = xs[0].shape[-3:]
    slots = parts * chunks
    width = wk.shape[1]
    size = width // heads
    each = members * residues
    rows = slots * each
    seqs = slots * members
    for k in range(slots):
        c, m = k % chunks, k // chunks
        start = sum(counts[:c])
        owner = m if counts[c] == 1 else me[0] ^ m
        block = xs[start][m] if counts[c] == 1 else xs[start + m][...]
        at = pl.ds(pl.multiple_of((owner * chunks + c) * each, each), each)
        x_s[at, :] = block.astype(F32).reshape(each, features)
    normed = standardize(x_s[...], gain[...])
    tiles = range(features // LANES)
    for i in tiles:
        n_s[i] = normed[:, i * LANES : (i + 1) * LANES]

    def strided(ref, r):
        return jnp.concatenate([ref[i, pl.ds(r, seqs, stride=residues), :] for i in tiles], 1)

    normed = jnp.concatenate([strided(n_s, r).astype(BF) for r in range(residues)], 0)
    scale = LOG2E / math.sqrt(size)
    keys = dot(normed, wk[...]).astype(BF)
    values = dot(wv_t[...], normed, NT).astype(BF)
    queries = (dot(wq_t[...], normed, NT) * scale).astype(BF)
    gates = jax.nn.sigmoid(dot(wg_t[...], normed, NT) + shift[...])
    join = max(1, LANES // seqs)
    span = join * seqs
    per = LANES // size
    ones = jnp.ones((ONES, span), BF)
    lane = lax.broadcasted_iota(jnp.int32, (1, span), 1) // seqs
    for t in range(residues // join):
        cols = slice(t * span, (t + 1) * span)
        attended = []
        crosses = []
        for h in range(heads):
            group = slice(h // per * LANES, (h // per + 1) * LANES)
            crosses.append(dot(keys[cols, group], head_mask(queries[group, cols], h % per, size)))
        spreads = []
        for crossed in crosses:
            scores = crossed[:seqs]
            for i in range(1, join):
                scores = jnp.where(lane == i, crossed[i * seqs : (i + 1) * seqs], scores)
            weights = jnp.exp2(scores - jnp.max(scores, axis=0, keepdims=True)).astype(BF)
            spread = [jnp.where(lane == i, weights, jnp.zeros_like(weights)) for i in range(join)]
            spreads.append(jnp.concatenate(spread, 0))
        for h, spread in enumerate(spreads):
            part = jnp.concatenate([values[h * size : (h + 1) * size, cols], ones], 0)
            total = dot(part, spread)
            gate = gates[h * size : (h + 1) * size, cols]
            attended.append((total[:size] / total[size : size + 1] * gate).astype(BF))
        update = dot(jnp.concatenate(attended, 0), wo[...], TN)
        for i in range(join):
            pick = pl.ds(t * join + i, seqs, stride=residues)
            for j in tiles:
                part = update[i * seqs : (i + 1) * seqs, j * LANES : (j + 1) * LANES]
                o_s[j, pick, :] = part
    block = (members * chunks, residues, features)
    for m in range(parts):
        owner = me[0] ^ m if split else m
        at = pl.ds(pl.multiple_of(owner * chunks * each, chunks * each), chunks * each)
        rows = x_s[at, :] + jnp.concatenate([o_s[j, at, :] for j in tiles], 1)
        if split:
            outs[m][...] = rows.astype(BF).reshape(block)
        else:
            outs[0][m] = rows.astype(BF).reshape(block)


def column_attention(me, xs, weights, parts, heads, first, residues, split):
    counts = tuple(len(blocks) for blocks in xs)
    chunks, flat = len(xs), [block for blocks in xs for block in blocks]
    members, _, features = flat[0].shape[-3:]
    step = 8
    rows = parts * chunks * members * step
    offset = first // step
    index = {
        3: lambda r, *_: (0, offset + r, 0),
        4: lambda r, *_: (0, 0, offset + r, 0),
    }
    block = (members * chunks, step, features)
    shape = (members * chunks, residues, features)
    if split:
        out_specs = [pl.BlockSpec(block, lambda r, *_: (0, r, 0))] * parts
        out_shape = [jax.ShapeDtypeStruct(shape, BF)] * parts
    else:
        out_specs = [pl.BlockSpec((parts,) + block, lambda r, *_: (0, 0, r, 0))]
        out_shape = [jax.ShapeDtypeStruct((parts,) + shape, BF)]
    grid_spec = pltpu.PrefetchScalarGridSpec(
        num_scalar_prefetch=1,
        grid=(residues // step,),
        in_specs=[
            pl.BlockSpec(b.shape[:-2] + (step, features), index[b.ndim]) for b in flat
        ]
        + [whole(w) for w in weights],
        out_specs=out_specs,
        scratch_shapes=[pltpu.VMEM((rows, features), F32)]
        + [pltpu.VMEM((features // LANES, rows, LANES), F32)] * 2,
    )
    return pl.pallas_call(
        functools.partial(column_kernel, counts, parts, heads, split),
        grid_spec=grid_spec,
        out_shape=out_shape,
        compiler_params=params(24 << 20),
        cost_estimate=cost(2 * rows // step * residues * features * features * 30, rows * 8),
        name="column_attention",
    )(me, *flat, *weights)


def assemble_kernel(count, me, *refs):
    blocks, out = refs[:count], refs[-1]
    for m in range(out.shape[1]):
        if count == 1:
            out[:, m, 0] = blocks[0][m].astype(F32)
        else:
            out[:, me[0] ^ m, 0] = blocks[m][...].astype(F32)


def assemble(me, blocks, parts, c, chunks, earlier):
    members, rows, features = blocks[0].shape[-3:]
    step = math.gcd(members, 4)
    held = [] if earlier is None else [earlier]
    if len(blocks) == 1:
        spec = pl.BlockSpec((parts, step, rows, features), lambda s, *_: (0, s, 0, 0))
    else:
        spec = pl.BlockSpec((step, rows, features), lambda s, *_: (s, 0, 0))
    grid_spec = pltpu.PrefetchScalarGridSpec(
        num_scalar_prefetch=1,
        grid=(members // step,),
        in_specs=[spec] * len(blocks) + [pl.BlockSpec(memory_space=pl.ANY)] * len(held),
        out_specs=pl.BlockSpec((step, parts, 1, rows, features), lambda s, *_: (s, 0, c, 0, 0)),
    )
    return pl.pallas_call(
        functools.partial(assemble_kernel, len(blocks)),
        grid_spec=grid_spec,
        out_shape=jax.ShapeDtypeStruct((members, parts, chunks, rows, features), F32),
        input_output_aliases={1 + len(blocks): 0} if held else {},
        compiler_params=params(16 << 20),
        cost_estimate=cost(0, parts * members * rows * features * 6),
        name="assemble",
    )(me, *blocks, *held)


def shards(
    alignment_embedding,
    unscaled_edge_prior,
    edge_prior_factor,
    horizontal_standardize_factor,
    horizontal_probe_lookup,
    horizontal_content_switch,
    horizontal_sigmoid_shift,
    horizontal_final_matrix,
    vertical_standardize_factor,
    vertical_probe_lookup,
    vertical_content_switch,
    vertical_sigmoid_shift,
    vertical_final_matrix,
):
    x = alignment_embedding
    members, count, features = x.shape
    heads = edge_prior_factor.shape[0]
    parts, blocks = lax.axis_size("seq"), lax.axis_size("res")
    seq, res = lax.axis_index("seq"), lax.axis_index("res")
    piece = unscaled_edge_prior.shape[2]

    def swap(array, axis, size, bits):
        return lax.ppermute(array, axis, [(i, i ^ bits) for i in range(size)])

    prior = jnp.swapaxes(unscaled_edge_prior, 1, 2)
    doubled = {0: prior}
    top = parts.bit_length() - 1
    first = swap(prior, "seq", parts, 1 << (top - 1))
    for b in reversed(range(1, top)):
        step = 1 << b
        for m in [m for m in doubled]:
            doubled[m ^ step] = first if b == top - 1 else swap(doubled[m], "seq", parts, step)
    near = [swap(x, "res", blocks, 1 << b) for b in range(blocks.bit_length() - 1)]
    order = sorted(doubled)
    order = order + [m ^ 1 for m in order]
    owners = jnp.stack([seq ^ m for m in order])
    per = count // piece
    place = ((owners // per) ^ res) * per + owners % per

    def prepared(gain, probe, switch, offset):
        return (
            gain[None],
            probe[1],
            switch[0].T,
            probe[0].T,
            switch[1].T,
            offset[:, None],
        )

    weights = prepared(
        horizontal_standardize_factor,
        horizontal_probe_lookup,
        horizontal_content_switch,
        horizontal_sigmoid_shift,
    )
    keys, values = [None] * blocks, [None] * blocks
    keys[0], values[0], queries, gates = project(x, weights, heads, True)
    near, queries = lax.optimization_barrier((near, queries))
    half = members // 2
    if blocks == 4:
        far = [
            swap(near[0][:half], "res", blocks, 2),
            swap(near[1][half:], "res", blocks, 1),
        ]
        x_slots = [x, near[0], near[1], jnp.concatenate(far, 0)]
    else:
        bits = {1 << b: rows for b, rows in enumerate(near)}
        x_slots = [x] + [
            bits[m] if m in bits else swap(x, "res", blocks, m) for m in range(1, blocks)
        ]
    for m in range(1, blocks):
        keys[m], values[m] = project(x_slots[m], weights, heads, False)
    priors = [doubled[m] for m in sorted(doubled)]
    last, keys = lax.optimization_barrier((priors[-1], keys))
    priors[-1] = last
    priors = priors + [swap(p, "seq", parts, 1) for p in priors]
    place = place.astype(jnp.int32)
    exchange = functools.partial(
        lax.all_to_all, axis_name="seq", split_axis=0, concat_axis=0, tiled=True
    )
    me = seq.astype(jnp.int32)[None]

    def deliver(blocks):
        if len(blocks) == 1:
            return [exchange(blocks[0])]
        return [blocks[0]] + [swap(blocks[m], "seq", parts, m) for m in range(1, parts)]

    columns = []
    chunk = members // ROW_CHUNKS
    for c in range(ROW_CHUNKS):
        mixed = row_attention(
            place,
            edge_prior_factor,
            me,
            x,
            queries,
            gates,
            horizontal_final_matrix,
            keys,
            values,
            priors,
            c * chunk,
            chunk,
            c == ROW_CHUNKS - 1,
        )
        columns.append(deliver(mixed))
    weights = prepared(
        vertical_standardize_factor,
        vertical_probe_lookup,
        vertical_content_switch,
        vertical_sigmoid_shift,
    ) + (vertical_final_matrix,)
    span = count // parts // COL_CHUNKS
    back = []
    for c in range(COL_CHUNKS):
        split = c == COL_CHUNKS - 1
        blocks = column_attention(me, columns, weights, parts, heads, c * span, span, split)
        back.append(deliver(blocks))
    out = None
    for c in range(COL_CHUNKS):
        out = assemble(me, back[c], parts, c, COL_CHUNKS, out)
    return out.reshape(members, count, features)


def solution(mesh):
    placed = (P("seq", "res", None), P(None, "res", "seq")) + (P(),) * 11
    return jax.shard_map(
        shards, mesh=mesh, in_specs=placed, out_specs=P("seq", "res", None), check_vma=False
    )
```
